32 devices in a mesh: tm: 4 (over z), gx: 4 (over y, x), gy: 2 (over core).
Axes of the slice: x: 2, y: 2, z: 4, core: 2. Of those that a mesh axis runs over, the one named last changes fastest.
Arguments:
- guesses: float32 [4, 64, 32, 256], P('tm', None, 'gx', 'gy'), may hold values from -6 to 6
- forcing: float32 [4, 64, 32, 256], P('tm', None, 'gx', 'gy'), may hold values from -4 to 4
- step_weight: float32 [16], replicated, may hold values from 0.25 to 1
- land_mask: int32 [32, 256], P('gx', 'gy'), may hold values 0 or 1
- fine_matrix: float32 [64, 64], replicated, may hold values from -1 to 1
- coupling: float32 [4, 64, 64], replicated, may hold values from -0.09375 to 0.09375
- coarse_matrix: float32 [64, 64], replicated, may hold values from -1 to 1
Outputs:
- updated_points: float32 [4, 64, 32, 256], P('tm', None, 'gx', 'gy')
- residual: float32 [4, 64, 32, 256], P('tm', None, 'gx', 'gy')
The draws below stay inside these ranges and needn't reach their ends.
All inputs are finite; a program needn't handle non-finite values. No bound on the sum of `land_mask` on one device may be relied on, other than what follows from the above.
Results may differ from the reference program's by a relative error of at most 0.0003.
Values sent between devices are 32-bit elements; how exact they have to be, the bound alone decides.
No kernel may reach another device: no remote copies, remote signals or barrier semaphores. Data moves between devices by JAX's collectives and lax.ppermute only.
A program may use at most 64 MiB of HBM per device.

```python
import math
import jax
import jax.numpy as jnp
from jax import lax

DOF = 64
FACTOR = 16
NC = 4
NBX = 32
NBY = 256


def rotation_matrix(key, decay_rates):
    half_size = decay_rates.shape[0] // 2
    key_size, key_sign = jax.random.split(key)
    magnitude = jax.random.uniform(key_size, (half_size,), jnp.float32, 0.3, 1.0)
    orientation = jnp.where(jax.random.bernoulli(key_sign, 0.5, (half_size,)), 1.0, -1.0)
    angles = magnitude * orientation
    cosine = jnp.cos(angles)
    sine_part = jnp.sin(angles)
    upper_rates = decay_rates[:half_size]
    lower_rates = decay_rates[half_size:]
    upper = jnp.concatenate([jnp.diag(upper_rates * cosine), jnp.diag(-upper_rates * sine_part)], 1)
    lower = jnp.concatenate([jnp.diag(lower_rates * sine_part), jnp.diag(lower_rates * cosine)], 1)
    return jnp.concatenate([upper, lower], 0).astype(jnp.float32)


def draw_coarse_matrix(key, part):
    key_slow, key_fast, key_pick, key_turn = jax.random.split(jax.random.fold_in(key, 11), 4)
    slow_rates = jnp.exp(jnp.log(0.1) * jax.random.uniform(key_slow, (DOF,), jnp.float32, 0.3, 1.0) / NC)
    fast_rates = jax.random.uniform(key_fast, (DOF,), jnp.float32, 0.85, 0.92)
    keeps_state = jax.random.bernoulli(key_pick, 0.5, (DOF,))
    decay_rates = jnp.where(keeps_state, slow_rates, fast_rates)
    return rotation_matrix(key_turn, decay_rates)


def draw_fine_matrix(key, part):
    key_rate, key_turn = jax.random.split(jax.random.fold_in(key, 23))
    decay_rates = jnp.exp(jax.random.uniform(key_rate, (DOF,), jnp.float32, jnp.log(0.5), jnp.log(0.98)))
    return rotation_matrix(key_turn, decay_rates)


def place_ends(entries, own_key, low, high):
    longest = entries.shape.index(max(entries.shape))
    spots = []
    for shift in (0, 1):
        where = [jax.random.randint(jax.random.fold_in(own_key, axis), (), 0, length) for axis, length in enumerate(entries.shape)]
        where[longest] = (where[longest] + shift) % entries.shape[longest]
        spots.append(tuple(where))
    return entries.at[spots[0]].set(low).at[spots[1]].set(high)


def levels(own_key, extent, cuts, smallest, top_value):
    gain, own = 1.0, jax.random.fold_in(own_key, 6)
    for dim, shards_of in cuts:
        draws = jnp.exp(jax.random.uniform(jax.random.fold_in(own, dim), (shards_of,), jnp.float32, smallest / len(cuts), top_value / len(cuts)))
        gain = gain * jnp.repeat(draws, extent[dim] // shards_of).reshape([-1 if axis == dim else 1 for axis in range(len(extent))])
    return gain


def centred(key, extent, width, limit, cuts=(), kind=jnp.bfloat16):
    values = jax.random.normal(key, extent, jnp.float32) * width
    if len(cuts) > 0:
        values = levels(key, extent, cuts, -0.22, 0.18) * values
    return jnp.clip(values, min=-limit, max=limit).astype(kind)


def setup_inputs(seed: int = 0) -> dict:
    key_of = jax.random.split(jax.random.key(seed), 8)
    guesses = centred(key_of[0], (NC, DOF, NBX, NBY), 1.0, 6.0, ((0, 4), (2, 4), (3, 2)), jnp.float32)
    forcing = centred(key_of[1], (NC, DOF, NBX, NBY), 0.5, 4.0, ((0, 4), (2, 4), (3, 2)), jnp.float32)
    step_weight = jnp.clip(jnp.exp(jax.random.uniform(key_of[2], (FACTOR,), jnp.float32, math.log(0.25), math.log(1.0))), 0.25, 1.0)
    land_mask = place_ends((jax.random.randint(key_of[3], (NBX, NBY), 0, 4) < 3).astype(jnp.int32), jax.random.fold_in(key_of[3], 1), 0, 1)
    fine_matrix = draw_fine_matrix(jax.random.fold_in(key_of[7], 71), 0)
    coupling = centred(key_of[5], (4, DOF, DOF), (DOF * DOF) ** -0.5, 0.09375, (), jnp.float32)
    coarse_matrix = draw_coarse_matrix(jax.random.fold_in(key_of[7], 71), 0)
    return {"guesses": guesses, "forcing": forcing, "step_weight": step_weight, "land_mask": land_mask, "fine_matrix": fine_matrix, "coupling": coupling, "coarse_matrix": coarse_matrix}


def propagate(matrix, field):
    return jnp.einsum("ij,jxy->ixy", matrix, field, precision=lax.Precision.HIGHEST)


def fine_step(adjoint, source, fine_matrix, coupling, ocean_mask):
    padded = jnp.pad(adjoint, ((0, 0), (1, 1), (1, 1)))
    summed = propagate(fine_matrix, padded[:, 1:-1, 1:-1])
    summed = summed + propagate(coupling[0], padded[:, :-2, 1:-1])
    summed = summed + propagate(coupling[1], padded[:, 2:, 1:-1])
    summed = summed + propagate(coupling[2], padded[:, 1:-1, :-2])
    summed = summed + propagate(coupling[3], padded[:, 1:-1, 2:])
    return (summed + source) * ocean_mask


def reference(guesses, forcing, step_weight, land_mask, fine_matrix, coupling, coarse_matrix):
    ocean_mask = land_mask.astype(jnp.float32)[None]
    successors = jnp.concatenate([guesses[1:], jnp.zeros_like(guesses[:1])], 0)

    def relax(inputs):
        start_point, guess, source = inputs
        adjoint = start_point
        for step_index in range(FACTOR - 1, 0, -1):
            adjoint = fine_step(adjoint, step_weight[step_index] * source, fine_matrix, coupling, ocean_mask)
        final = fine_step(adjoint, step_weight[0] * source, fine_matrix, coupling, ocean_mask)
        return final - guess * ocean_mask

    residual = lax.map(relax, (successors, guesses, forcing))

    def backward(correction, residual_point):
        correction = propagate(coarse_matrix, correction) * ocean_mask + residual_point
        return correction, correction

    initial = jnp.zeros_like(guesses[0])
    unused, corrections = lax.scan(backward, initial, residual, reverse=True)
    return guesses + corrections, residual
```

```python
import jax
import jax.numpy as jnp
from jax import lax
from jax.experimental import pallas as pl
from jax.experimental.pallas import tpu as pltpu
from jax.sharding import PartitionSpec as P

F32 = jnp.float32
LANES = 128


def lane_of(shape):
    return lax.broadcasted_iota(jnp.int32, shape, len(shape) - 1)


def roll(value, shift, axis=1):
    shift %= value.shape[axis]
    return value if shift == 0 else pltpu.roll(value, shift, axis)


class Plan:
    def __init__(self, mesh_sizes, dof, rows, cols, steps):
        self.planes, self.gx, self.gy = mesh_sizes
        self.dof, self.rows, self.cols, self.halo = dof, rows, cols, steps
        self.strip = cols // self.gx
        self.window = self.strip + 2 * steps
        self.pack = LANES // self.window
        self.groups = rows // self.pack
        self.width = self.gx * self.window
        self.back = LANES // self.strip
        self.back_groups = rows // self.back
        assert self.gy == 2 and cols == LANES and self.window * self.pack == LANES
        assert rows * self.halo == LANES and rows == 8 and self.width % LANES == 0
        assert self.strip >= self.halo and self.back_groups * self.back == rows


def call(kernel, outs, n_in, smem=(), scratch=()):
    specs = [
        pl.BlockSpec(memory_space=pltpu.SMEM if i in smem else pltpu.VMEM) for i in range(n_in)
    ]
    out_specs = [pl.BlockSpec(memory_space=pltpu.VMEM) for _ in outs]
    single = len(outs) == 1
    return pl.pallas_call(
        kernel,
        in_specs=specs,
        out_specs=out_specs[0] if single else out_specs,
        out_shape=outs[0] if single else outs,
        scratch_shapes=list(scratch),
    )


def edge_kernel(plan):
    h, n = plan.halo, plan.cols

    def packed(row_of, half):
        lane = lane_of((1, LANES))
        result = None
        for x in range(plan.rows):
            row = row_of(x)
            low = roll(row, h * x)
            high = roll(row, h * x - (n - h))
            piece = jnp.where(half == 0, high, low)
            result = piece if x == 0 else jnp.where(lane >= h * x, piece, result)
        return result

    def kernel(half_ref, forcing_ref, guess_ref, land_ref, edge_f_ref, edge_g_ref):
        half = half_ref[0]
        edge_f_ref[0 : plan.dof] = packed(lambda x: forcing_ref[0, :, x, :], half)
        edge_f_ref[plan.dof :] = land_ref[...].astype(F32)
        edge_g_ref[...] = packed(lambda x: guess_ref[0, :, x, :], half)

    return call(
        kernel,
        [
            jax.ShapeDtypeStruct((plan.dof + plan.rows, LANES), F32),
            jax.ShapeDtypeStruct((plan.dof, LANES), F32),
        ],
        4,
        smem=(0,),
    )


def windows(plan, row, below, above):
    h = plan.halo
    lane = lane_of((1, LANES))
    found = []
    for q in range(plan.gx):
        source = row
        if q == 0:
            source = jnp.where(lane >= LANES - h, below, source)
        if q == plan.gx - 1:
            source = jnp.where(lane < h, above, source)
        found.append((source, h - plan.strip * q))
    return found


def pack_kernel(plan, with_land):
    h, w = plan.halo, plan.window

    def kernel(half_ref, field_ref, edge_ref, *rest):
        half = half_ref[0]
        out_ref = rest[-1]
        lane = lane_of((1, LANES))
        edge = edge_ref[0 : plan.dof]
        below_edge = jnp.where(half == 1, edge, 0.0)
        above_edge = jnp.where(half == 0, edge, 0.0)

        def of_row(x):
            below = roll(below_edge, LANES - h - h * x)
            above = roll(above_edge, -h * x)
            return windows(plan, field_ref[0, :, x, :], below, above)

        for j in range(plan.groups):
            parts = [of_row(j + plan.groups * m) for m in range(plan.pack)]
            for q in range(plan.gx):
                piece = None
                for m in range(plan.pack):
                    source, shift = parts[m][q]
                    moved = roll(source, shift + w * m)
                    piece = moved if m == 0 else jnp.where(lane >= w * m, moved, piece)
                out_ref[q, plan.dof * j : plan.dof * (j + 1)] = piece
        if with_land:
            land = rest[0][...].astype(F32)
            other = edge_ref[plan.dof :]
            below = jnp.where(half == 1, other, 0.0)
            above = jnp.where(half == 0, other, 0.0)
            for q, (source, shift) in enumerate(windows(plan, land, below, above)):
                piece = None
                for m in range(plan.pack):
                    moved = roll(roll(source, shift + w * m), -plan.groups * m, 0)
                    piece = moved if m == 0 else jnp.where(lane >= w * m, moved, piece)
                out_ref[q, plan.dof * plan.groups :] = piece

    extra = plan.rows if with_land else 0
    shape = (plan.gx, plan.dof * plan.groups + extra, LANES)
    return call(kernel, [jax.ShapeDtypeStruct(shape, F32)], 4 if with_land else 3, smem=(0,))


def relax_kernel(plan, steps):
    dof, w, rows, h = plan.dof, plan.window, plan.rows, plan.halo
    vregs = plan.width // LANES
    per = LANES // w

    def assembled(piece_ref, j, row0, count):
        m = j // plan.groups
        base = row0 + count * (j % plan.groups)
        lane = lane_of((1, LANES))
        halves = []
        for v in range(vregs):
            value = None
            for u in range(per):
                part = piece_ref[v * per + u, base : base + count]
                part = roll(part, w * (u - m))
                value = part if u == 0 else jnp.where(lane >= w * u, part, value)
            halves.append(value)
        return jnp.concatenate(halves, axis=1)

    def kernel(weight_ref, matrix_ref, f_ref, a_ref, out_ref, state_ref, f_all, mask_all, acc, wst, est):
        lane = lane_of((1, plan.width))

        def put(slot, j, value):
            high = value.astype(jnp.bfloat16)
            low = (value - high.astype(F32)).astype(jnp.bfloat16)
            state_ref[slot, j, 0:dof] = high
            state_ref[slot, j, dof : 2 * dof] = low

        for j in range(rows):
            put(0, j, assembled(a_ref, j, 0, dof))
            f_all[j] = assembled(f_ref, j, 0, dof)
            mask_all[j] = jnp.broadcast_to(
                assembled(f_ref, j, dof * plan.groups, 1), (8, plan.width)
            )

        def rolled(value, shift):
            parts = [
                roll(value[:, LANES * v : LANES * (v + 1)], shift) for v in range(vregs)
            ]
            return jnp.concatenate(parts, axis=1)

        def step(slot, weight, finish):
            for j in range(rows):
                high = state_ref[slot, j, 0:dof]
                both = state_ref[slot, j]
                out = jnp.dot(
                    matrix_ref[...],
                    jnp.concatenate([both, high], axis=0),
                    preferred_element_type=F32,
                )
                wst[j] = out[dof : 2 * dof]
                est[j] = out[2 * dof : 3 * dof]
                acc[j] = (
                    out[0:dof]
                    + rolled(out[3 * dof : 4 * dof], 1)
                    + rolled(out[4 * dof : 5 * dof], -1)
                )
            for j in range(rows):
                if j > 0:
                    west = wst[j - 1]
                else:
                    west = jnp.where(lane >= w, pltpu.roll(wst[rows - 1], w, 1), 0.0)
                if j < rows - 1:
                    east = est[j + 1]
                else:
                    east = jnp.where(
                        lane < plan.width - w, pltpu.roll(est[0], plan.width - w, 1), 0.0
                    )
                total = acc[j] + west + east + weight * f_all[j]
                finish(j, total * mask_all[j, 0:1])

        def two(i, carry):
            k = steps - 1 - 2 * i
            step(0, weight_ref[k], lambda j, v: put(1, j, v))
            step(1, weight_ref[k - 1], lambda j, v: put(0, j, v))
            return carry

        lax.fori_loop(0, steps // 2 - 1, two, 0)
        step(0, weight_ref[1], lambda j, v: put(1, j, v))

        def emit(j, value):
            f_all[j] = value

        step(1, weight_ref[0], emit)
        s = plan.strip
        small = lane_of((1, LANES))
        for q in range(plan.gx):
            v, u = divmod(q, per)
            for group in range(plan.back_groups):
                piece = None
                for m in range(plan.back):
                    part = f_all[group * plan.back + m, :, LANES * v : LANES * (v + 1)]
                    part = roll(part, s * m - (w * u + h))
                    piece = part if m == 0 else jnp.where(small >= s * m, part, piece)
                out_ref[q, dof * group : dof * (group + 1)] = piece

    tile = (rows, dof, plan.width)
    return call(
        kernel,
        [jax.ShapeDtypeStruct((plan.gx, dof * plan.back_groups, LANES), F32)],
        4,
        smem=(0,),
        scratch=[
            pltpu.VMEM((2, rows, 2 * dof, plan.width), jnp.bfloat16),
            pltpu.VMEM(tile, F32),
            pltpu.VMEM((rows, 8, plan.width), F32),
            pltpu.VMEM(tile, F32),
            pltpu.VMEM(tile, F32),
            pltpu.VMEM(tile, F32),
        ],
    )


def residual_kernel(plan):
    dof, s = plan.dof, plan.strip

    def kernel(piece_ref, guess_ref, land_ref, out_ref):
        lane = lane_of((1, LANES))
        mask = land_ref[...].astype(F32)
        for x in range(plan.rows):
            group, m = divmod(x, plan.back)
            row = None
            for q in range(plan.gx):
                part = roll(piece_ref[q, dof * group : dof * (group + 1)], s * (q - m))
                row = part if q == 0 else jnp.where(lane >= s * q, part, row)
            out_ref[0, :, x, :] = row - guess_ref[0, :, x, :] * mask[x : x + 1]

    shape = (1, dof, plan.rows, LANES)
    return call(kernel, [jax.ShapeDtypeStruct(shape, F32)], 3)


def stacked_matrix(fine_matrix, coupling):
    full = jnp.concatenate([fine_matrix[None], coupling], axis=0)
    full = full.reshape(-1, full.shape[-1])
    rounded = lax.reduce_precision(full, 8, 7)
    high = rounded.astype(jnp.bfloat16)
    low = (full - rounded).astype(jnp.bfloat16)
    return jnp.concatenate([high, high, low], axis=1)


def earlier(count):
    return [(t, t - 1) for t in range(1, count)]


def per_device(guesses, forcing, step_weight, land_mask, fine_matrix, coupling, coarse_matrix):
    planes, gx, gy = (lax.axis_size(name) for name in ("tm", "gx", "gy"))
    _, dof, rows, cols = guesses.shape
    steps = step_weight.shape[0]
    plan = Plan((planes, gx, gy), dof, rows, cols, steps)
    half = lax.axis_index("gy").astype(jnp.int32)[None]

    start = lax.ppermute(guesses, "tm", earlier(planes))
    edge_f, edge_g = edge_kernel(plan)(half, forcing, guesses, land_mask)
    edge_f = lax.ppermute(edge_f, "gy", [(0, 1), (1, 0)])
    edge_g = lax.ppermute(
        edge_g,
        ("tm", "gy"),
        [(t * gy + c, (t - 1) * gy + 1 - c) for t in range(1, planes) for c in range(gy)],
    )
    f_pieces = pack_kernel(plan, True)(half, forcing, edge_f, land_mask)
    f_pieces = lax.all_to_all(f_pieces, "gx", 0, 0, tiled=True)
    a_pieces = pack_kernel(plan, False)(half, start, edge_g)
    a_pieces = lax.all_to_all(a_pieces, "gx", 0, 0, tiled=True)
    relaxed = relax_kernel(plan, steps)(
        step_weight, stacked_matrix(fine_matrix, coupling), f_pieces, a_pieces
    )
    relaxed = lax.all_to_all(relaxed, "gx", 0, 0, tiled=True)
    residual = residual_kernel(plan)(relaxed, guesses, land_mask)

    mask = land_mask.astype(F32)[None]

    def advance(field):
        moved = jnp.einsum("ij,jxy->ixy", coarse_matrix, field, precision=lax.Precision.HIGHEST)
        return moved * mask + residual[0]

    def turn(_, incoming):
        return lax.ppermute(advance(incoming), "tm", earlier(planes))

    incoming = lax.fori_loop(0, planes - 1, turn, jnp.zeros_like(residual[0]))
    return guesses + advance(incoming)[None], residual


def solution(mesh):
    return jax.shard_map(
        per_device,
        mesh=mesh,
        in_specs=(
            P("tm", None, "gx", "gy"),
            P("tm", None, "gx", "gy"),
            P(),
            P("gx", "gy"),
            P(),
            P(),
            P(),
        ),
        out_specs=(P("tm", None, "gx", "gy"), P("tm", None, "gx", "gy")),
        check_vma=False,
    )
```

```python
import jax
import jax.numpy as jnp
from jax import lax
from jax.experimental import pallas as pl
from jax.experimental.pallas import tpu as pltpu
from jax.sharding import PartitionSpec as P


F32 = jnp.float32
LANES = 128


def lane_of(shape):
    return lax.broadcasted_iota(jnp.int32, shape, len(shape) - 1)


def roll(value, shift, axis=1):
    shift %= value.shape[axis]
    return value if shift == 0 else pltpu.roll(value, shift, axis)


class Plan:
    def __init__(self, mesh_sizes, dof, rows, cols, steps):
        self.planes, self.gx, self.gy = mesh_sizes
        self.dof, self.rows, self.cols, self.halo = dof, rows, cols, steps
        self.strip = cols // self.gx
        self.window = self.strip + 2 * steps
        self.pack = LANES // self.window
        self.groups = rows // self.pack
        self.width = self.gx * self.window
        self.back = LANES // self.strip
        self.back_groups = rows // self.back
        self.square = self.planes == self.gx
        assert self.gy == 2 and cols == LANES and self.window * self.pack == LANES
        assert self.gx & (self.gx - 1) == 0 and steps % 2 == 0
        assert rows * self.halo == LANES and rows == 8 and self.width % LANES == 0
        assert self.strip >= self.halo and self.back_groups * self.back == rows


def call(kernel, outs, n_in, smem=(), scratch=(), leave=(), hbm=()):
    specs = [
        pl.BlockSpec(memory_space=pltpu.SMEM if i in smem else pltpu.VMEM) for i in range(n_in)
    ]
    out_specs = [pl.BlockSpec(memory_space=pltpu.VMEM) for _ in outs]
    outs = [
        out if i in leave else pltpu.VMEM(out.shape, out.dtype) for i, out in enumerate(outs)
    ]
    single = len(outs) == 1
    run = pl.pallas_call(
        kernel,
        in_specs=specs,
        out_specs=out_specs[0] if single else out_specs,
        out_shape=outs[0] if single else outs,
        scratch_shapes=list(scratch),
    )

    def placed(*args):
        return run(
            *(
                arg if i in smem or i in hbm else pltpu.with_memory_space_constraint(arg, pltpu.VMEM)
                for i, arg in enumerate(args)
            )
        )

    return placed


def edge_kernel(plan):
    h, n = plan.halo, plan.cols

    def packed(row_of, half):
        lane = lane_of((1, LANES))
        result = None
        for x in range(plan.rows):
            row = row_of(x)
            low = roll(row, h * x)
            high = roll(row, h * x - (n - h))
            piece = jnp.where(half == 0, high, low)
            result = piece if x == 0 else jnp.where(lane >= h * x, piece, result)
        return result

    def kernel(place_ref, forcing_ref, guess_ref, land_ref, edge_f_ref, edge_g_ref):
        half = place_ref[2]
        edge_f_ref[0 : plan.dof] = packed(lambda x: forcing_ref[0, :, x, :], half)
        edge_f_ref[plan.dof :] = land_ref[...].astype(F32)
        edge_g_ref[...] = packed(lambda x: guess_ref[0, :, x, :], half)

    return call(
        kernel,
        [
            jax.ShapeDtypeStruct((plan.dof + plan.rows, LANES), F32),
            jax.ShapeDtypeStruct((plan.dof, LANES), F32),
        ],
        4,
        smem=(0,),
        hbm=(1, 2, 3),
    )


def windows(plan, row, below, above):
    h = plan.halo
    lane = lane_of((1, LANES))
    found = []
    for q in range(plan.gx):
        source = row
        if q == 0:
            source = jnp.where(lane >= LANES - h, below, source)
        if q == plan.gx - 1:
            source = jnp.where(lane < h, above, source)
        found.append((source, h - plan.strip * q))
    return found


def sides(shape, count):
    return [jax.ShapeDtypeStruct(shape, F32) for _ in range(count)]


def pack_kernel(plan, with_land):
    h, w, dof = plan.halo, plan.window, plan.dof
    base = dof * plan.groups

    def kernel(place_ref, field_ref, edge_ref, *rest):
        half = place_ref[2]
        outs, all_ref = rest[-1 - plan.gx : -1], rest[-1]
        lane = lane_of((1, LANES))
        edge = edge_ref[0:dof]
        below_edge = jnp.where(half == 1, edge, 0.0)
        above_edge = jnp.where(half == 0, edge, 0.0)

        def of_row(x):
            below = roll(below_edge, LANES - h - h * x)
            above = roll(above_edge, -h * x)
            return windows(plan, field_ref[0, :, x, :], below, above)

        for j in range(plan.groups):
            parts = [of_row(j + plan.groups * m) for m in range(plan.pack)]
            for q in range(plan.gx):
                piece = None
                for m in range(plan.pack):
                    source, shift = parts[m][q]
                    moved = roll(source, shift + w * m)
                    piece = moved if m == 0 else jnp.where(lane >= w * m, moved, piece)
                all_ref[q, dof * j : dof * (j + 1)] = piece
        if with_land:
            land_ref, guess_ref = rest[0], rest[1]
            land = land_ref[...].astype(F32)
            other = edge_ref[dof:]
            below = jnp.where(half == 1, other, 0.0)
            above = jnp.where(half == 0, other, 0.0)
            for q, (source, shift) in enumerate(windows(plan, land, below, above)):
                piece = None
                for m in range(plan.pack):
                    moved = roll(roll(source, shift + w * m), -plan.groups * m, 0)
                    piece = moved if m == 0 else jnp.where(lane >= w * m, moved, piece)
                all_ref[q, base : base + plan.rows] = piece
            for group in range(plan.back_groups):
                start = base + plan.rows + dof * group
                for q in range(plan.gx):
                    piece = None
                    for m in range(plan.back):
                        part = roll(
                            guess_ref[0, :, group * plan.back + m, :], plan.strip * (m - q)
                        )
                        piece = part if m == 0 else jnp.where(lane >= plan.strip * m, part, piece)
                    all_ref[q, start : start + dof] = piece
        for k in range(plan.gx):
            outs[k][...] = all_ref[place_ref[1] ^ k]

    extra = plan.rows + dof * plan.back_groups if with_land else 0
    shape = (base + extra, LANES)
    return call(
        kernel,
        sides(shape, plan.gx),
        5 if with_land else 3,
        smem=(0,),
        scratch=[pltpu.VMEM((plan.gx,) + shape, F32)],
    )


def relax_kernel(plan, steps):
    dof, w, rows, h, gx, s = plan.dof, plan.window, plan.rows, plan.halo, plan.gx, plan.strip
    vregs = plan.width // LANES
    per = LANES // w
    base = dof * plan.groups

    def assembled(piece_of, j, row0, count):
        m = j // plan.groups
        first = row0 + count * (j % plan.groups)
        lane = lane_of((1, LANES))
        halves = []
        for v in range(vregs):
            value = None
            for u in range(per):
                part = piece_of(v * per + u)[first : first + count]
                part = roll(part, w * (u - m))
                value = part if u == 0 else jnp.where(lane >= w * u, part, value)
            halves.append(value)
        return jnp.concatenate(halves, axis=1)

    def kernel(place_ref, weight_ref, matrix_ref, *refs):
        f_in, a_in, refs = refs[:gx], refs[gx : 2 * gx], refs[2 * gx :]
        home, across, land_ref, refs = (
            refs[:gx],
            refs[gx : gx + plan.gx],
            refs[2 * gx],
            refs[2 * gx + 1 :],
        )
        state_ref, f_all, mask_all, acc, wst, est, f_raw, a_raw, r_all, land_all = refs
        lane = lane_of((1, plan.width))
        small = lane_of((1, LANES))

        def put(slot, j, value):
            high = value.astype(jnp.bfloat16)
            low = (value - high.astype(F32)).astype(jnp.bfloat16)
            state_ref[slot, j, 0:dof] = high
            state_ref[slot, j, dof : 2 * dof] = low

        for k in range(gx):
            f_raw[place_ref[1] ^ k] = f_in[k][...]
            a_raw[place_ref[1] ^ k] = a_in[k][...]
        for j in range(rows):
            put(0, j, assembled(lambda q: a_raw.at[q], j, 0, dof))
            f_all[j] = assembled(lambda q: f_raw.at[q], j, 0, dof)
            mask_all[j] = jnp.broadcast_to(
                assembled(lambda q: f_raw.at[q], j, base, 1), (8, plan.width)
            )

        def rolled(value, shift):
            parts = [
                roll(value[:, LANES * v : LANES * (v + 1)], shift) for v in range(vregs)
            ]
            return jnp.concatenate(parts, axis=1)

        def step(slot, weight, finish):
            for j in range(rows):
                high = state_ref[slot, j, 0:dof]
                both = state_ref[slot, j]
                out = jnp.dot(
                    matrix_ref[...],
                    jnp.concatenate([both, high], axis=0),
                    preferred_element_type=F32,
                )
                wst[j] = out[dof : 2 * dof]
                est[j] = out[2 * dof : 3 * dof]
                acc[j] = (
                    out[0:dof]
                    + rolled(out[3 * dof : 4 * dof], 1)
                    + rolled(out[4 * dof : 5 * dof], -1)
                )
            for j in range(rows):
                if j > 0:
                    west = wst[j - 1]
                else:
                    west = jnp.where(lane >= w, pltpu.roll(wst[rows - 1], w, 1), 0.0)
                if j < rows - 1:
                    east = est[j + 1]
                else:
                    east = jnp.where(
                        lane < plan.width - w, pltpu.roll(est[0], plan.width - w, 1), 0.0
                    )
                total = acc[j] + west + east + weight * f_all[j]
                finish(j, total * mask_all[j, 0:1])

        def two(i, carry):
            k = steps - 1 - 2 * i
            step(0, weight_ref[k], lambda j, v: put(1, j, v))
            step(1, weight_ref[k - 1], lambda j, v: put(0, j, v))
            return carry

        lax.fori_loop(0, steps // 2 - 1, two, 0)
        step(0, weight_ref[1], lambda j, v: put(1, j, v))

        def emit(j, value):
            f_all[j] = value

        step(1, weight_ref[0], emit)
        for q in range(gx):
            v, u = divmod(q, per)
            lanes = slice(LANES * v, LANES * (v + 1))
            for group in range(plan.back_groups):
                piece = None
                land = None
                for m in range(plan.back):
                    j = group * plan.back + m
                    shift = s * m - (w * u + h)
                    part = roll(f_all[j, :, lanes], shift)
                    mask = roll(mask_all[j, :, lanes], shift)
                    piece = part if m == 0 else jnp.where(small >= s * m, part, piece)
                    land = mask if m == 0 else jnp.where(small >= s * m, mask, land)
                start = base + rows + dof * group
                guess = f_raw[q, start : start + dof]
                r_all[q, dof * group : dof * (group + 1)] = piece - guess * land[0:1]
                land_all[q, 8 * group : 8 * (group + 1)] = land
        for k in range(gx):
            home[k][...] = r_all[place_ref[1] ^ k]
        if plan.square:
            for k in range(gx):
                across[k][...] = r_all[place_ref[0] ^ k]
            land_ref[...] = land_all[place_ref[0]]

    tile = (rows, dof, plan.width)
    piece = (dof * plan.back_groups, LANES)
    extra = rows + dof * plan.back_groups
    return call(
        kernel,
        sides(piece, 2 * gx) + sides((8 * plan.back_groups, LANES), 1),
        3 + 2 * gx,
        smem=(0, 1),
        scratch=[
            pltpu.VMEM((2, rows, 2 * dof, plan.width), jnp.bfloat16),
            pltpu.VMEM(tile, F32),
            pltpu.VMEM((rows, 8, plan.width), F32),
            pltpu.VMEM(tile, F32),
            pltpu.VMEM(tile, F32),
            pltpu.VMEM(tile, F32),
            pltpu.VMEM((gx, base + extra, LANES), F32),
            pltpu.VMEM((gx, base, LANES), F32),
            pltpu.VMEM((gx,) + piece, F32),
            pltpu.VMEM((gx, 8 * plan.back_groups, LANES), F32),
        ],
    )


def unpacked(plan, pieces, x, lane):
    group, m = divmod(x, plan.back)
    row = None
    for q in range(plan.gx):
        part = pieces[q, plan.dof * group : plan.dof * (group + 1)]
        part = roll(part, plan.strip * (q - m))
        row = part if q == 0 else jnp.where(lane >= plan.strip * q, part, row)
    return row


def residual_kernel(plan):
    def kernel(place_ref, guess_ref, *refs):
        out_ref, sum_ref, all_ref = refs[-3:]
        lane = lane_of((1, LANES))
        for k in range(plan.gx):
            all_ref[place_ref[1] ^ k] = refs[k][...]
        for x in range(plan.rows):
            row = unpacked(plan, all_ref, x, lane)
            out_ref[0, :, x, :] = row
            sum_ref[0, :, x, :] = guess_ref[0, :, x, :] + row

    shape = (1, plan.dof, plan.rows, LANES)
    return call(
        kernel,
        sides(shape, 2),
        2 + plan.gx,
        smem=(0,),
        leave=(0,),
        scratch=[pltpu.VMEM((plan.gx, plan.dof * plan.back_groups, LANES), F32)],
    )


def coarse_kernel(plan):
    dof, n = plan.dof, plan.back_groups

    def kernel(place_ref, matrix_ref, land_ref, *refs):
        outs, r_all, e_all = refs[plan.planes : -2], refs[-2], refs[-1]
        for k in range(plan.planes):
            r_all[place_ref[0] ^ k] = refs[k][...]
        e_all[plan.planes - 1] = jnp.zeros_like(e_all[0])
        carry = None
        for t in range(plan.planes - 2, -1, -1):
            fresh = [r_all[t + 1, dof * v : dof * (v + 1)] for v in range(n)]
            if carry is not None:
                fresh = [a + b for a, b in zip(fresh, carry)]
            value = jnp.concatenate(fresh, axis=1)
            high = value.astype(jnp.bfloat16)
            low = (value - high.astype(F32)).astype(jnp.bfloat16)
            moved = jnp.dot(
                matrix_ref[...],
                jnp.concatenate([high, low, high], axis=0),
                preferred_element_type=F32,
            )
            carry = []
            for v in range(n):
                part = moved[:, LANES * v : LANES * (v + 1)] * land_ref[8 * v : 8 * v + 1]
                e_all[t, dof * v : dof * (v + 1)] = part
                carry.append(part)
        for k in range(plan.gx):
            outs[k][...] = e_all[place_ref[1] ^ k]

    piece = (dof * n, LANES)
    return call(
        kernel,
        sides(piece, plan.gx),
        3 + plan.planes,
        smem=(0,),
        scratch=[pltpu.VMEM((plan.planes,) + piece, F32)] * 2,
    )


def update_kernel(plan):
    def kernel(place_ref, sum_ref, *refs):
        out_ref, all_ref = refs[-2:]
        lane = lane_of((1, LANES))
        for k in range(plan.gx):
            all_ref[place_ref[0] ^ k] = refs[k][...]
        for x in range(plan.rows):
            out_ref[0, :, x, :] = sum_ref[0, :, x, :] + unpacked(plan, all_ref, x, lane)

    shape = (1, plan.dof, plan.rows, LANES)
    return call(
        kernel,
        sides(shape, 1),
        2 + plan.gx,
        smem=(0,),
        leave=(0,),
        scratch=[pltpu.VMEM((plan.gx, plan.dof * plan.back_groups, LANES), F32)],
    )


def split_matrix(full):
    rounded = lax.reduce_precision(full, 8, 7)
    high = rounded.astype(jnp.bfloat16)
    low = (full - rounded).astype(jnp.bfloat16)
    return jnp.concatenate([high, high, low], axis=1)


def earlier(count):
    return [(t, t - 1) for t in range(1, count)]


def swapped(pieces, axis):
    count = lax.axis_size(axis)
    return [pieces[0]] + [
        lax.ppermute(pieces[k], axis, [(i, i ^ k) for i in range(count)])
        for k in range(1, count)
    ]


def per_device(guesses, forcing, step_weight, land_mask, fine_matrix, coupling, coarse_matrix):
    planes, gx, gy = (lax.axis_size(name) for name in ("tm", "gx", "gy"))
    _, dof, rows, cols = guesses.shape
    steps = step_weight.shape[0]
    plan = Plan((planes, gx, gy), dof, rows, cols, steps)
    place = jnp.stack([lax.axis_index(name) for name in ("tm", "gx", "gy")]).astype(jnp.int32)

    start = lax.ppermute(guesses, "tm", earlier(planes))
    edge_f, edge_g = edge_kernel(plan)(place, forcing, guesses, land_mask)
    edge_f = lax.ppermute(edge_f, "gy", [(0, 1), (1, 0)])
    edge_g = lax.ppermute(
        edge_g,
        ("tm", "gy"),
        [(t * gy + c, (t - 1) * gy + 1 - c) for t in range(1, planes) for c in range(gy)],
    )
    f_pieces = pack_kernel(plan, True)(place, forcing, edge_f, land_mask, guesses)
    f_pieces = swapped(f_pieces, "gx")
    a_pieces = swapped(pack_kernel(plan, False)(place, start, edge_g), "gx")
    full = jnp.concatenate([fine_matrix[None], coupling], axis=0).reshape(-1, dof)
    *relaxed, land_piece = relax_kernel(plan, steps)(
        place, step_weight, split_matrix(full), *f_pieces, *a_pieces
    )
    home, across = relaxed[:gx], relaxed[gx:]
    if plan.square:
        across = swapped(across, "tm")
        home = swapped(home, "gx")
        residual, total = residual_kernel(plan)(place, guesses, *home)
        parts = coarse_kernel(plan)(place, split_matrix(coarse_matrix), land_piece, *across)
        parts = [
            lax.ppermute(
                parts[k],
                ("tm", "gx"),
                [(p * gx + i, (i ^ k) * gx + p) for p in range(planes) for i in range(gx)],
            )
            for k in range(gx)
        ]
        return update_kernel(plan)(place, total, *parts), residual

    residual, total = residual_kernel(plan)(place, guesses, *swapped(home, "gx"))
    mask = land_mask.astype(F32)[None]

    def advance(field):
        moved = jnp.einsum("ij,jxy->ixy", coarse_matrix, field, precision=lax.Precision.HIGHEST)
        return moved * mask

    def turn(_, incoming):
        return lax.ppermute(advance(incoming) + residual[0], "tm", earlier(planes))

    incoming = lax.fori_loop(0, planes - 1, turn, jnp.zeros_like(residual[0]))
    return total + advance(incoming)[None], residual


def solution(mesh):
    return jax.shard_map(
        per_device,
        mesh=mesh,
        in_specs=(
            P("tm", None, "gx", "gy"),
            P("tm", None, "gx", "gy"),
            P(),
            P("gx", "gy"),
            P(),
            P(),
            P(),
        ),
        out_specs=(P("tm", None, "gx", "gy"), P("tm", None, "gx", "gy")),
        check_vma=False,
    )
```
